256 devices in a mesh: ia: 8 (over z_lo, core), ja: 32 (over y, x, z_hi).
Axes of the slice: x: 4, y: 4, z: 8 (z_hi: 2, z_lo: 4; z = z_hi * 4 + z_lo), core: 2. Of those that a mesh axis runs over, the one named last changes fastest.
Arguments:
- slab_rows: bfloat16 [256, 768, 128], P('ia', 'ja'), may hold values from -6 to 6
- column_rows: bfloat16 [512, 768, 128], P('ja', 'ia'), may hold values from -6 to 6
- pair_tile: bfloat16 [256, 512, 128], P('ia', 'ja'), may hold values from -6 to 6
- cotangent: bfloat16 [256, 512, 128], P('ia', 'ja'), may hold values from -6 to 6
- weights_left: bfloat16 [128, 256], replicated, may hold values from -0.5 to 0.5
- weights_right: bfloat16 [128, 256], replicated, may hold values from -0.5 to 0.5
- gate_weight: bfloat16 [128, 128], replicated, may hold values from -0.5 to 0.5
- out_weight: bfloat16 [128, 128], replicated, may hold values from -0.5 to 0.5
- input_gain: float32 [128], replicated, may hold values from 0.1 to 1.9
- input_bias: float32 [128], replicated, may hold values from -3 to 3
- update_gain: float32 [128], replicated, may hold values from 0.1 to 1.9
- update_bias: float32 [128], replicated, may hold values from -3 to 3
Outputs:
- update: bfloat16 [256, 512, 128], P('ia', 'ja')
- grad_slab: bfloat16 [256, 768, 128], P('ia', 'ja')
- grad_columns: bfloat16 [512, 768, 128], P('ja', 'ia')
- grad_tile: bfloat16 [256, 512, 128], P('ia', 'ja')
The draws below stay inside these ranges and needn't reach their ends.
All inputs are finite; a program needn't handle non-finite values.
Results may differ from the reference program's by a relative error of at most 0.018.
Values may be sent and summed in bfloat16 or wider, within the bound.
No kernel may reach another device: no remote copies, remote signals or barrier semaphores. Data moves between devices by JAX's collectives and lax.ppermute only.
A program may use at most 128 MiB of HBM per device.

```python
import jax
import jax.numpy as jnp
from jax import lax

CZ = 128
CH = 128
I_DEV = 32
J_DEV = 16
SLAB = 256
COLS = 512
RES = 768
N_IA = 8
N_JA = 32


def level_of(own_key, extent, pieces, smallest, top_value):
    loudness = 1.0
    for axis_at, blocks in pieces:
        draws = jax.random.uniform(jax.random.fold_in(jax.random.fold_in(own_key, 6), axis_at), (blocks,), jnp.float32, smallest / len(pieces), top_value / len(pieces))
        loudness = loudness * jnp.repeat(jnp.exp(draws), extent[axis_at] // blocks).reshape((-1,) + (1,) * (len(extent) - 1 - axis_at))
    return loudness


def noise(own_key, extent, width, reach, shards=(), dtype=jnp.bfloat16):
    factor_of = level_of(own_key, extent, shards, -0.22, 0.18) if shards else 1.0
    result = jax.random.normal(own_key, extent, jnp.float32) * width * factor_of
    return jnp.minimum(jnp.maximum(result, -reach), reach).astype(dtype)


def setup_inputs(seed: int = 0) -> dict:
    streams_of = jax.random.split(jax.random.key(seed), 13)
    slab_rows = noise(streams_of[0], (SLAB, RES, CZ), 1.0, 6.0, ((0, 8), (1, 32)))
    column_rows = noise(streams_of[1], (COLS, RES, CZ), 1.0, 6.0, ((0, 32), (1, 8)))
    pair_tile = noise(streams_of[2], (SLAB, COLS, CZ), 1.0, 6.0, ((0, 8), (1, 32)))
    cotangent = noise(streams_of[3], (SLAB, COLS, CZ), 1.0, 6.0, ((0, 8), (1, 32)))
    weights_left = noise(streams_of[4], (CZ, 2 * CH), CZ ** -0.5, 0.5)
    weights_right = noise(streams_of[5], (CZ, 2 * CH), CZ ** -0.5, 0.5)
    gate_weight = noise(streams_of[6], (CZ, CZ), CZ ** -0.5, 0.5)
    out_weight = noise(streams_of[7], (CH, CZ), CH ** -0.5, 0.5)
    input_gain = jnp.clip(1.0 + 0.18 * jax.random.normal(streams_of[8], (CZ,), jnp.float32), 0.1, 1.9)
    input_bias = noise(streams_of[9], (CZ,), 0.5, 3.0, (), jnp.float32)
    update_gain = jnp.clip(1.0 + 0.18 * jax.random.normal(streams_of[10], (CH,), jnp.float32), 0.1, 1.9)
    update_bias = noise(streams_of[11], (CH,), 0.5, 3.0, (), jnp.float32)
    return {"slab_rows": slab_rows, "column_rows": column_rows, "pair_tile": pair_tile, "cotangent": cotangent, "weights_left": weights_left, "weights_right": weights_right, "gate_weight": gate_weight, "out_weight": out_weight, "input_gain": input_gain, "input_bias": input_bias, "update_gain": update_gain, "update_bias": update_bias}


epsilon = 1e-05

def normalize(values, gain, bias):
    values = values.astype(jnp.float32)
    centre = lax.optimization_barrier(jnp.mean(values, axis=-1, keepdims=True))
    shifted = values - centre
    inverse = lax.rsqrt(lax.optimization_barrier(jnp.mean(shifted * shifted, axis=-1, keepdims=True)) + epsilon)
    scaled = shifted * inverse
    return (scaled * gain + bias, scaled, inverse)

def norm_back(scaled, inverse, grad_out, gain):
    grad_hat = grad_out * gain
    first_mean = lax.optimization_barrier(jnp.mean(grad_hat, axis=-1, keepdims=True))
    second_mean = lax.optimization_barrier(jnp.mean(grad_hat * scaled, axis=-1, keepdims=True))
    return inverse * (grad_hat - first_mean - scaled * second_mean)

def project(rows, weights, input_gain, input_bias):
    normed, scaled, inverse = normalize(rows, input_gain, input_bias)
    hidden = jnp.dot(normed.astype(jnp.bfloat16), weights, preferred_element_type=jnp.float32)
    half_width = weights.shape[1] // 2
    linear = hidden[..., :half_width]
    sigma = jax.nn.sigmoid(hidden[..., half_width:])
    return ((sigma * linear).astype(jnp.bfloat16), linear, sigma, scaled, inverse)

def project_back(grad_edge, linear, sigma, scaled, inverse, weights, input_gain):
    joined = jnp.concatenate([grad_edge * sigma, grad_edge * linear * sigma * (1.0 - sigma)], axis=-1)
    grad_norm = jnp.dot(joined.astype(jnp.bfloat16), weights.T, preferred_element_type=jnp.float32)
    return norm_back(scaled, inverse, grad_norm, input_gain).astype(jnp.bfloat16)

def reference(slab_rows, column_rows, pair_tile, cotangent, weights_left, weights_right, gate_weight, out_weight, input_gain, input_bias, update_gain, update_bias):
    left, lin_left, sig_left, scaled_left, inv_left = project(slab_rows, weights_left, input_gain, input_bias)
    right, lin_right, sig_right, scaled_right, inv_right = project(column_rows, weights_right, input_gain, input_bias)
    triangle = jnp.einsum('ikc,jkc->ijc', left.astype(jnp.float32), right.astype(jnp.float32))
    tri_norm, tri_scaled, tri_inverse = normalize(triangle, update_gain, update_bias)
    outer = jnp.dot(tri_norm.astype(jnp.bfloat16), out_weight, preferred_element_type=jnp.float32)
    tile_norm, tile_scaled, tile_inverse = normalize(pair_tile, input_gain, input_bias)
    gate_linear = jnp.dot(tile_norm.astype(jnp.bfloat16), gate_weight, preferred_element_type=jnp.float32)
    gate = jax.nn.sigmoid(gate_linear)
    update = (gate * outer).astype(jnp.bfloat16)
    grad_update = cotangent.astype(jnp.float32)
    grad_outer = (grad_update * gate).astype(jnp.bfloat16)
    grad_gate = (grad_update * outer * gate * (1.0 - gate)).astype(jnp.bfloat16)
    grad_tnorm = jnp.dot(grad_outer, out_weight.T, preferred_element_type=jnp.float32)
    grad_tri = norm_back(tri_scaled, tri_inverse, grad_tnorm, update_gain).astype(jnp.bfloat16)
    grad_pnorm = jnp.dot(grad_gate, gate_weight.T, preferred_element_type=jnp.float32)
    grad_tile = norm_back(tile_scaled, tile_inverse, grad_pnorm, input_gain).astype(jnp.bfloat16)
    slab_count = left.shape[0]
    col_count = right.shape[0]
    res_count = left.shape[1]
    hidden_count = left.shape[2]
    tri_by_cols = jnp.transpose(grad_tri.reshape(slab_count, N_JA, J_DEV, hidden_count), (1, 0, 2, 3))
    right_blocks = right.reshape(N_JA, J_DEV, res_count, hidden_count)

    def add_left(running, blocks):
        tri_block, right_block = blocks
        partial_sum = jnp.einsum('ijc,jkc->ikc', tri_block.astype(jnp.float32), right_block.astype(jnp.float32))
        rounded = lax.optimization_barrier(partial_sum.astype(jnp.bfloat16))
        return (running + rounded.astype(jnp.float32), None)
    grad_left, unused_left = lax.scan(add_left, jnp.zeros((slab_count, res_count, hidden_count), jnp.float32), (tri_by_cols, right_blocks))
    tri_by_rows = grad_tri.reshape(N_IA, I_DEV, col_count, hidden_count)
    left_blocks = left.reshape(N_IA, I_DEV, res_count, hidden_count)

    def add_right(running, blocks):
        tri_block, left_block = blocks
        partial_sum = jnp.einsum('ijc,ikc->jkc', tri_block.astype(jnp.float32), left_block.astype(jnp.float32))
        rounded = lax.optimization_barrier(partial_sum.astype(jnp.bfloat16))
        return (running + rounded.astype(jnp.float32), None)
    grad_right, unused_right = lax.scan(add_right, jnp.zeros((col_count, res_count, hidden_count), jnp.float32), (tri_by_rows, left_blocks))
    grad_slab = project_back(grad_left, lin_left, sig_left, scaled_left, inv_left, weights_left, input_gain)
    grad_columns = project_back(grad_right, lin_right, sig_right, scaled_right, inv_right, weights_right, input_gain)
    return (update, grad_slab, grad_columns, grad_tile)
```

```python
import jax
import jax.numpy as jnp
from jax import lax
from jax.sharding import Mesh
from jax.sharding import PartitionSpec as P

IA = ("zl", "co")
JA = ("y", "x", "zh")
SPLIT = ("zl", "y", "x", "zh")

epsilon = 1e-05


def normalize(values, gain, bias):
    values = values.astype(jnp.float32)
    centre = jnp.mean(values, axis=-1, keepdims=True)
    shifted = values - centre
    inverse = lax.rsqrt(jnp.mean(shifted * shifted, axis=-1, keepdims=True) + epsilon)
    scaled = shifted * inverse
    return (scaled * gain + bias, scaled, inverse)


def norm_back(scaled, inverse, grad_out, gain):
    grad_hat = grad_out * gain
    first_mean = jnp.mean(grad_hat, axis=-1, keepdims=True)
    second_mean = jnp.mean(grad_hat * scaled, axis=-1, keepdims=True)
    return inverse * (grad_hat - first_mean - scaled * second_mean)


def project(rows, weights, input_gain, input_bias):
    normed, scaled, inverse = normalize(rows, input_gain, input_bias)
    hidden = jnp.dot(normed.astype(jnp.bfloat16), weights, preferred_element_type=jnp.float32)
    half_width = weights.shape[1] // 2
    linear = hidden[..., :half_width]
    sigma = jax.nn.sigmoid(hidden[..., half_width:])
    return ((sigma * linear).astype(jnp.bfloat16), linear, sigma, scaled, inverse)


def project_back(grad_edge, linear, sigma, scaled, inverse, weights, input_gain):
    joined = jnp.concatenate(
        [grad_edge * sigma, grad_edge * linear * sigma * (1.0 - sigma)], axis=-1
    )
    grad_norm = jnp.dot(joined.astype(jnp.bfloat16), weights.T, preferred_element_type=jnp.float32)
    return norm_back(scaled, inverse, grad_norm, input_gain).astype(jnp.bfloat16)


def shuffled(array):
    return lax.all_to_all(array, SPLIT, 0, 0, tiled=True)


def swapped(array):
    return lax.ppermute(array, "co", [(0, 1), (1, 0)])


def dot32(spec, a, b):
    return jnp.einsum(spec, a, b, preferred_element_type=jnp.float32)


def shards(
    slab_rows,
    column_rows,
    pair_tile,
    cotangent,
    weights_left,
    weights_right,
    gate_weight,
    out_weight,
    input_gain,
    input_bias,
    update_gain,
    update_bias,
):
    core = lax.axis_index("co")
    left, lin_left, sig_left, scaled_left, inv_left = project(
        slab_rows, weights_left, input_gain, input_bias
    )
    right, lin_right, sig_right, scaled_right, inv_right = project(
        column_rows, weights_right, input_gain, input_bias
    )
    left_sent = jnp.transpose(left, (2, 1, 0)).reshape(128, 768)
    right_sent = jnp.transpose(right, (2, 0, 1)).reshape(128, 1536)
    got = shuffled(jnp.concatenate([left_sent, right_sent], axis=1))
    left_got = got[:, :768].reshape(4, 4, 2, 4, 24, 32)
    left_ki = jnp.transpose(left_got, (2, 1, 3, 4, 0, 5)).reshape(2, 384, 128)
    right_jk = jnp.transpose(got[:, 768:].reshape(4, 512, 96), (1, 0, 2)).reshape(512, 384)
    right_other = swapped(right_jk)
    left_own = jnp.where(core == 0, left_ki[0], left_ki[1])
    left_other = jnp.where(core == 0, left_ki[1], left_ki[0])
    tri = dot32("ki,jk->ij", left_own, right_jk) + dot32("ki,jk->ij", left_other, right_other)
    tri_sent = jnp.transpose(tri.astype(jnp.bfloat16).reshape(4, 32, 32, 16), (0, 2, 1, 3))
    tri_got = shuffled(tri_sent.reshape(128, 512))
    running = jnp.transpose(tri_got.astype(jnp.float32)).reshape(32, 16, 128)

    tri_norm, tri_scaled, tri_inverse = normalize(running, update_gain, update_bias)
    outer = jnp.dot(tri_norm.astype(jnp.bfloat16), out_weight, preferred_element_type=jnp.float32)
    tile_norm, tile_scaled, tile_inverse = normalize(pair_tile, input_gain, input_bias)
    gate_linear = jnp.dot(
        tile_norm.astype(jnp.bfloat16), gate_weight, preferred_element_type=jnp.float32
    )
    gate = jax.nn.sigmoid(gate_linear)
    update = (gate * outer).astype(jnp.bfloat16)
    grad_update = cotangent.astype(jnp.float32)
    grad_outer = (grad_update * gate).astype(jnp.bfloat16)
    grad_gate = (grad_update * outer * gate * (1.0 - gate)).astype(jnp.bfloat16)
    grad_tnorm = jnp.dot(grad_outer, out_weight.T, preferred_element_type=jnp.float32)
    grad_tri = norm_back(tri_scaled, tri_inverse, grad_tnorm, update_gain).astype(jnp.bfloat16)
    grad_pnorm = jnp.dot(grad_gate, gate_weight.T, preferred_element_type=jnp.float32)
    grad_tile = norm_back(tile_scaled, tile_inverse, grad_pnorm, input_gain).astype(jnp.bfloat16)

    d_got = shuffled(jnp.transpose(grad_tri.reshape(512, 128)))
    d_ij = jnp.transpose(d_got.reshape(4, 32, 32, 16), (0, 2, 1, 3)).reshape(128, 512)
    d_right_other = dot32("ij,ki->jk", d_ij, left_other).astype(jnp.bfloat16)
    d_right_come = swapped(d_right_other)
    d_left_own = dot32("jk,ij->ki", right_jk, d_ij)
    d_left_other = dot32("jk,ij->ki", right_other, d_ij)
    d_right = (dot32("ij,ki->jk", d_ij, left_own) + d_right_come.astype(jnp.float32)).astype(
        jnp.bfloat16
    )
    d_left = jnp.stack(
        [
            jnp.where(core == 0, d_left_own, d_left_other),
            jnp.where(core == 0, d_left_other, d_left_own),
        ]
    ).astype(jnp.bfloat16)
    d_left = jnp.transpose(d_left.reshape(2, 4, 4, 24, 4, 32), (4, 1, 0, 2, 3, 5)).reshape(128, 768)
    d_right = jnp.transpose(d_right.reshape(512, 4, 96), (1, 0, 2)).reshape(128, 1536)
    back = shuffled(jnp.concatenate([d_left, d_right], axis=1))
    grad_left = jnp.transpose(back[:, :768].reshape(128, 24, 32), (2, 1, 0)).astype(jnp.float32)
    grad_right = jnp.transpose(back[:, 768:].reshape(128, 16, 96), (1, 2, 0)).astype(jnp.float32)
    grad_slab = project_back(
        grad_left, lin_left, sig_left, scaled_left, inv_left, weights_left, input_gain
    )
    grad_columns = project_back(
        grad_right, lin_right, sig_right, scaled_right, inv_right, weights_right, input_gain
    )
    return (update, grad_slab, grad_columns, grad_tile)


def solution(mesh):
    finer = Mesh(mesh.devices.reshape(4, 2, 4, 4, 2), ("zl", "co", "y", "x", "zh"))
    row_spec = P(IA, JA, None)
    column_spec = P(JA, IA, None)
    in_specs = (row_spec, column_spec, row_spec, row_spec) + (P(),) * 8
    return jax.shard_map(
        shards,
        mesh=finer,
        in_specs=in_specs,
        out_specs=(row_spec, row_spec, column_spec, row_spec),
        check_vma=False,
    )
```

```python
import functools

import jax
import jax.numpy as jnp
from jax import lax
from jax.experimental import pallas as pl
from jax.experimental.pallas import tpu as pltpu
from jax.sharding import Mesh
from jax.sharding import PartitionSpec as P

IA = ("zl", "co")
JA = ("y", "x", "zh")
SPLIT = ("zl", "y", "x", "zh")

epsilon = 1e-05
F32 = jnp.float32
BF16 = jnp.bfloat16


def stats(values):
    centre = jnp.mean(values, axis=-1, keepdims=True)
    shifted = values - centre
    inverse = lax.rsqrt(jnp.mean(shifted * shifted, axis=-1, keepdims=True) + epsilon)
    return shifted * inverse, inverse


def norm_back(scaled, inverse, grad_out, gain):
    grad_hat = grad_out * gain
    first_mean = jnp.mean(grad_hat, axis=-1, keepdims=True)
    second_mean = jnp.mean(grad_hat * scaled, axis=-1, keepdims=True)
    return inverse * (grad_hat - first_mean - scaled * second_mean)


def dot(a, b, dims=((1,), (0,))):
    return lax.dot_general(a, b, (dims, ((), ())), preferred_element_type=F32)


def edges(rows, weights, gain, bias):
    scaled, inverse = stats(rows.astype(F32))
    hidden = dot((scaled * gain + bias).astype(BF16), weights)
    return hidden[:, :128], jax.nn.sigmoid(hidden[:, 128:]), scaled, inverse


def lane_group(shape):
    return lax.broadcasted_iota(jnp.int32, shape, 1) // 32


def moved(block, source, target):
    shift = ((target - source) * 32) % 128
    return block if shift == 0 else pltpu.roll(block, shift, 1)


def project_kernel(slab, column, w_left, w_right, gain, bias, out, left_rows, chunks):
    g, b = gain[...], bias[...]
    for step in range(8):
        rows = pl.ds(step * 96, 96)
        linear, sigma, _, _ = edges(slab[rows, :], w_left[...], g, b)
        left_rows[rows, :] = sigma * linear
    for r in range(24):
        left_part = left_rows[pl.ds(r, 32, stride=24), :]
        if r < 16:
            linear, sigma, _, _ = edges(column[pl.ds(r * 96, 96), :], w_right[...], g, b)
            right_part = sigma * linear
        else:
            right_part = jnp.zeros((96, 128), F32)
        block = jnp.concatenate([right_part, left_part], axis=0)
        chunks[pl.ds(r, 128, stride=24), :] = block.T
    out[...] = chunks[...].astype(BF16)


def right_of(chunk):
    rows = chunk.astype(F32).reshape(32, 24, 128)[:, :16, :].reshape(512, 128)
    return rows.astype(BF16)


def padded(rows):
    return jnp.concatenate([rows, jnp.zeros((32, 128), BF16)], axis=0)


def left_block(left, zl, core):
    start = pl.multiple_of((2 * zl + core) * 96, 32)
    return padded(left[pl.ds(start, 96), :])


def first_product_kernel(core, got, left, right, partial):
    group = lane_group((768, 128))
    merged = None
    for zl in range(4):
        chunk = got[pl.ds(zl * 768, 768), :]
        piece = moved(chunk.astype(F32), 3, zl)
        merged = piece if merged is None else jnp.where(group == zl, piece, merged)
        right[pl.ds(zl * 512, 512), :] = right_of(chunk)
    left[...] = merged.astype(BF16)
    total = None
    for zl in range(4):
        term = dot(right[pl.ds(zl * 512, 512), :], left_block(left, zl, core[0]))
        total = term if total is None else total + term
    partial[...] = total


def second_product_kernel(core, come, left, partial, right, out, total):
    acc = partial[...]
    for zl in range(4):
        chunk = right_of(come[pl.ds(zl * 768, 768), :])
        right[pl.ds(zl * 512, 512), :] = chunk
        acc = acc + dot(chunk, left_block(left, zl, 1 - core[0]))
    total[...] = acc
    group = lane_group((128, 128))
    parts = [total[pl.ds(jl, 128, stride=4), :] for jl in range(4)]
    for zl in range(4):
        merged = moved(parts[0], zl, 0)
        for jl in range(1, 4):
            merged = jnp.where(group == jl, moved(parts[jl], zl, jl), merged)
        out[pl.ds(zl * 128, 128), :] = merged.astype(BF16)


def gate_kernel(tile, cotangent, gate_w, out_w, gain, bias, u_gain, gate_out, eg_out, rows, cots):
    scaled, _ = stats(tile[...].astype(F32))
    gate = jax.nn.sigmoid(
        dot((scaled * gain[...] + bias[...]).astype(BF16), gate_w[...])
    )
    gate_out[...] = gate
    grad_outer = (cotangent[...].astype(F32) * gate).astype(BF16)
    rows[...] = dot(grad_outer, out_w[...], ((1,), (1,))) * u_gain[...]
    for jh in range(4):
        block = jnp.concatenate(
            [rows[pl.ds(4 * jh + jl, 32, stride=16), :] for jl in range(4)], axis=0
        )
        eg_out[pl.ds(jh * 128, 128), :] = block.T


def tri_back_kernel(tri, eg, out, tri_rows, d_rows):
    tri_rows[...] = tri[...].astype(F32)
    for jh in range(4):
        value = tri_rows[pl.ds(jh, 128, stride=4), :]
        centre = jnp.mean(value, axis=0, keepdims=True)
        shifted = value - centre
        inverse = lax.rsqrt(jnp.mean(shifted * shifted, axis=0, keepdims=True) + epsilon)
        scaled = shifted * inverse
        grad_hat = eg[pl.ds(jh * 128, 128), :]
        first_mean = jnp.mean(grad_hat, axis=0, keepdims=True)
        second_mean = jnp.mean(grad_hat * scaled, axis=0, keepdims=True)
        d_rows[pl.ds(jh, 128, stride=4), :] = inverse * (
            grad_hat - first_mean - scaled * second_mean
        )
    out[...] = d_rows[...].astype(BF16)


def tile_kernel(
    tri, tile, cotangent, gate_in, gate_w, out_w, gain, bias, u_gain, u_bias,
    update, grad_tile, tri_rows, run_rows,
):
    tri_rows[...] = tri[...].astype(F32)
    for jh in range(4):
        block = tri_rows[pl.ds(jh, 128, stride=4), :].T
        for jl in range(4):
            run_rows[pl.ds(4 * jh + jl, 32, stride=16), :] = block[jl * 32 : jl * 32 + 32, :]
    tri_scaled, _ = stats(run_rows[...])
    outer = dot((tri_scaled * u_gain[...] + u_bias[...]).astype(BF16), out_w[...])
    gate = gate_in[...]
    update[...] = (gate * outer).astype(BF16)
    grad_gate = (cotangent[...].astype(F32) * outer * gate * (1.0 - gate)).astype(BF16)
    grad_norm = dot(grad_gate, gate_w[...], ((1,), (1,)))
    scaled, inverse = stats(tile[...].astype(F32))
    grad_tile[...] = norm_back(scaled, inverse, grad_norm, gain[...]).astype(BF16)


def third_product_kernel(core, d_got, left, d_tri, d_right, d_rows):
    group = lane_group((128, 128))
    parts = [d_got[pl.ds(zl * 128, 128), :].astype(F32) for zl in range(4)]
    for jl in range(4):
        merged = moved(parts[0], jl, 0)
        for zl in range(1, 4):
            merged = jnp.where(group == zl, moved(parts[zl], jl, zl), merged)
        d_rows[pl.ds(jl, 128, stride=4), :] = merged
    d_now = d_rows[...].astype(BF16)
    d_tri[...] = d_now
    for zl in range(4):
        block = dot(d_now, left_block(left, zl, 1 - core[0]), ((1,), (1,)))
        d_right[pl.ds(zl * 512, 512), :] = block.astype(BF16)


def fourth_product_kernel(core, d_tri, right_own, right_other, d_left):
    d_t = d_tri[...].astype(F32).T.astype(BF16)
    for zl in range(4):
        for right, which in ((right_own, core[0]), (right_other, 1 - core[0])):
            block = dot(d_t, right[pl.ds(zl * 512, 512), :]).T
            start = pl.multiple_of((2 * zl + which) * 96, 32)
            d_left[pl.ds(start, 96), :] = block[:96, :]


def fifth_product_kernel(core, d_tri, left, come, d_left, out):
    d_now = d_tri[...]
    is_left = lane_group((768, 128)) == 3
    for zl in range(4):
        block = dot(d_now, left_block(left, zl, core[0]), ((1,), (1,)))
        block = block + come[pl.ds(zl * 512, 512), :].astype(F32)
        block = jnp.concatenate(
            [block.reshape(32, 16, 128), jnp.zeros((32, 8, 128), F32)], axis=1
        ).reshape(768, 128)
        merged = jnp.where(is_left, moved(d_left[...], zl, 3), block)
        out[pl.ds(zl * 768, 768), :] = merged.astype(BF16)


def edges_back(grad_edge, rows, weights, gain, bias):
    linear, sigma, scaled, inverse = edges(rows, weights, gain, bias)
    joined = jnp.concatenate(
        [grad_edge * sigma, grad_edge * linear * sigma * (1.0 - sigma)], axis=1
    )
    grad_norm = dot(joined.astype(BF16), weights, ((1,), (1,)))
    return norm_back(scaled, inverse, grad_norm, gain).astype(BF16)


def project_back_kernel(
    back, slab, column, w_left, w_right, gain, bias, grad_slab, grad_column, chunks, left_rows
):
    g, b = gain[...], bias[...]
    chunks[...] = back[...].astype(F32)
    for r in range(24):
        block = chunks[pl.ds(r, 128, stride=24), :].T
        left_rows[pl.ds(r, 32, stride=24), :] = block[96:, :]
        if r < 16:
            rows = pl.ds(r * 96, 96)
            grad_column[rows, :] = edges_back(block[:96, :], column[rows, :], w_right[...], g, b)
    for step in range(8):
        rows = pl.ds(step * 96, 96)
        grad_slab[rows, :] = edges_back(left_rows[rows, :], slab[rows, :], w_left[...], g, b)


VMEM = pl.BlockSpec(memory_space=pltpu.VMEM)
SMEM = pl.BlockSpec(memory_space=pltpu.SMEM)


def run(kernel, name, outs, scratch, *args, flops=100_000_000, moved_bytes=2_000_000):
    return pl.pallas_call(
        kernel,
        name=name,
        out_shape=[jax.ShapeDtypeStruct(s, t) for s, t in outs],
        in_specs=[SMEM if a.dtype == jnp.int32 else VMEM for a in args],
        out_specs=[VMEM] * len(outs),
        scratch_shapes=[pltpu.VMEM((n, 128), F32) for n in scratch],
        cost_estimate=pl.CostEstimate(
            flops=flops, bytes_accessed=moved_bytes, transcendentals=0
        ),
    )(*args)


def shuffled(array):
    rows = array.shape[0] // 128
    return lax.all_to_all(array.reshape(128, rows, 128), SPLIT, 0, 0, tiled=True).reshape(
        array.shape
    )


def swapped(array):
    return lax.ppermute(array, "co", [(0, 1), (1, 0)])


def shards(
    slab_rows,
    column_rows,
    pair_tile,
    cotangent,
    weights_left,
    weights_right,
    gate_weight,
    out_weight,
    input_gain,
    input_bias,
    update_gain,
    update_bias,
):
    core = lax.axis_index("co").astype(jnp.int32).reshape(1)
    slab = slab_rows.reshape(768, 128)
    column = column_rows.reshape(1536, 128)
    tile = pair_tile.reshape(512, 128)
    cots = cotangent.reshape(512, 128)
    gain, bias, u_gain, u_bias = (
        v.reshape(1, 128) for v in (input_gain, input_bias, update_gain, update_bias)
    )
    (sent,) = run(
        project_kernel, "project", [((3072, 128), BF16)], [768, 3072],
        slab, column, weights_left, weights_right, gain, bias,
    )
    got = shuffled(sent)
    gate, eg = run(
        gate_kernel, "gate", [((512, 128), F32)] * 2, [512, 512],
        tile, cots, gate_weight, out_weight, gain, bias, u_gain,
    )
    come = swapped(got)
    left, right_own, partial = run(
        first_product_kernel, "product_one",
        [((768, 128), BF16), ((2048, 128), BF16), ((512, 128), F32)], [], core, got,
    )
    right_other, tri_sent = run(
        second_product_kernel, "product_two",
        [((2048, 128), BF16), ((512, 128), BF16)], [512], core, come, left, partial,
    )
    tri = shuffled(tri_sent)
    (d_sent,) = run(tri_back_kernel, "tri_back", [((512, 128), BF16)], [512, 512], tri, eg)
    d_got = shuffled(d_sent)
    update, grad_tile = run(
        tile_kernel, "tile", [((512, 128), BF16)] * 2, [512, 512],
        tri, tile, cots, gate, gate_weight, out_weight, gain, bias, u_gain, u_bias,
    )
    d_tri, d_right_other = run(
        third_product_kernel, "product_three",
        [((512, 128), BF16), ((2048, 128), BF16)], [512], core, d_got, left,
    )
    d_right_come = swapped(d_right_other)
    (d_left,) = run(
        fourth_product_kernel, "product_four", [((768, 128), F32)], [],
        core, d_tri, right_own, right_other,
    )
    (back_sent,) = run(
        fifth_product_kernel, "product_five", [((3072, 128), BF16)], [],
        core, d_tri, left, d_right_come, d_left,
    )
    back = shuffled(back_sent)
    grad_slab, grad_column = run(
        project_back_kernel, "project_back",
        [((768, 128), BF16), ((1536, 128), BF16)], [3072, 768],
        back, slab, column, weights_left, weights_right, gain, bias,
    )
    return (
        update.reshape(pair_tile.shape),
        grad_slab.reshape(slab_rows.shape),
        grad_column.reshape(column_rows.shape),
        grad_tile.reshape(pair_tile.shape),
    )


def solution(mesh):
    finer = Mesh(mesh.devices.reshape(4, 2, 4, 4, 2), ("zl", "co", "y", "x", "zh"))
    row_spec = P(IA, JA, None)
    column_spec = P(JA, IA, None)
    in_specs = (row_spec, column_spec, row_spec, row_spec) + (P(),) * 8
    return jax.shard_map(
        shards,
        mesh=finer,
        in_specs=in_specs,
        out_specs=(row_spec, row_spec, column_spec, row_spec),
        check_vma=False,
    )
```

```python
import functools

import jax
import jax.numpy as jnp
from jax import lax
from jax.experimental import pallas as pl
from jax.experimental.pallas import tpu as pltpu
from jax.sharding import Mesh
from jax.sharding import PartitionSpec as P

IA = ("zl", "co")
JA = ("y", "x", "zh")
SPLIT = ("zl", "y", "x", "zh")

epsilon = 1e-05
F32 = jnp.float32
BF16 = jnp.bfloat16


ROWS = 18


def stats(values):
    centre = jnp.mean(values, axis=-1, keepdims=True)
    shifted = values - centre
    inverse = lax.rsqrt(jnp.mean(shifted * shifted, axis=-1, keepdims=True) + epsilon)
    return shifted * inverse, inverse


def norm_back(scaled, inverse, grad_out, gain):
    grad_hat = grad_out * gain
    first_mean = jnp.mean(grad_hat, axis=-1, keepdims=True)
    second_mean = jnp.mean(grad_hat * scaled, axis=-1, keepdims=True)
    return inverse * (grad_hat - first_mean - scaled * second_mean)


def dot(a, b, dims=((1,), (0,))):
    return lax.dot_general(a, b, (dims, ((), ())), preferred_element_type=F32)


def edges(rows, weights, gain, bias):
    scaled, inverse = stats(rows.astype(F32))
    hidden = dot((scaled * gain + bias).astype(BF16), weights)
    return hidden[:, :128], jax.nn.sigmoid(hidden[:, 128:]), scaled, inverse


def lane_group(shape):
    return lax.broadcasted_iota(jnp.int32, shape, 1) // 32


def moved(block, source, target):
    shift = ((target - source) * 32) % 128
    return block if shift == 0 else pltpu.roll(block, shift, 1)


def tail_k(r, g):
    return 16 + 4 * (r - 16) + g


def project_kernel(gain, bias, w_left, slab, w_right, column, out, left_rows, chunks):
    g, b = gain()[...], bias()[...]
    w_left, slab = w_left(), slab()
    for step in range(8):
        rows = pl.ds(step * 96, 96)
        linear, sigma, _, _ = edges(slab[rows, :], w_left[...], g, b)
        left_rows[rows, :] = sigma * linear

    def left_part(k):
        return left_rows[pl.ds(k, 32, stride=24), :]

    w_right, column = w_right(), column()
    for r in range(ROWS):
        if r < 16:
            linear, sigma, _, _ = edges(column[pl.ds(r * 96, 96), :], w_right[...], g, b)
            parts = [sigma * linear, left_part(r)]
        else:
            parts = [left_part(tail_k(r, q)) for q in range(4)]
        chunks[pl.ds(r, 128, stride=ROWS), :] = jnp.concatenate(parts, axis=0).T
    out[...] = chunks[...].astype(BF16)


def gathered(parts, sources, targets, group):
    merged = None
    for part, source, target in zip(parts, sources, targets):
        piece = moved(part, source, target)
        merged = piece if merged is None else jnp.where(group == target, piece, merged)
    return merged


def padded(rows):
    return jnp.concatenate([rows, jnp.zeros((32, 128), BF16)], axis=0)


def left_block(left, zl, core):
    start = pl.multiple_of((2 * zl + core) * 96, 32)
    return padded(left[pl.ds(start, 96), :])


def first_product_kernel(core, got, left, right, partial, rows, left_rows):
    group = lane_group((32, 128))
    rows[...] = got[...].astype(F32)
    for r in range(ROWS):
        parts = [rows[pl.ds(zl * 32 * ROWS + r, 32, stride=ROWS), :] for zl in range(4)]
        if r < 16:
            for zl in range(4):
                right[pl.ds(zl * 512 + r * 32, 32), :] = parts[zl].astype(BF16)
            left_rows[pl.ds(r, 32, stride=24), :] = gathered(parts, (3,) * 4, range(4), group)
        else:
            for q in range(4):
                left_rows[pl.ds(tail_k(r, q), 32, stride=24), :] = gathered(
                    parts, (q,) * 4, range(4), group
                )
    left[...] = left_rows[...].astype(BF16)
    total = None
    for zl in range(4):
        term = dot(right[pl.ds(zl * 512, 512), :], left_block(left, zl, core[0]))
        total = term if total is None else total + term
    partial[...] = total


def second_product_kernel(core, come, left, partial, right, out, rows, sent):
    rows[...] = come[...].astype(F32)
    acc = partial[...]
    for zl in range(4):
        for r in range(16):
            right[pl.ds(zl * 512 + r * 32, 32), :] = rows[
                pl.ds(zl * 32 * ROWS + r, 32, stride=ROWS), :
            ].astype(BF16)
        acc = acc + dot(right[pl.ds(zl * 512, 512), :], left_block(left, zl, 1 - core[0]))
    group = lane_group((32, 128))
    for jh in range(4):
        parts = [acc[(4 * jh + jl) * 32 : (4 * jh + jl + 1) * 32, :] for jl in range(4)]
        for zl in range(4):
            sent[pl.ds(zl * 128 + jh, 32, stride=4), :] = gathered(
                parts, (zl,) * 4, range(4), group
            )
    out[...] = sent[...].astype(BF16)


def gate_of(tile, gate_w, gain, bias):
    scaled, inverse = stats(tile[...].astype(F32))
    hidden = dot((scaled * gain[...] + bias[...]).astype(BF16), gate_w[...])
    return jax.nn.sigmoid(hidden), scaled, inverse


def gate_kernel(gain, bias, u_gain, gate_w, tile, out_w, cotangent, eg_out, rows):
    gate, _, _ = gate_of(tile(), gate_w(), gain(), bias())
    grad_outer = (cotangent()[...].astype(F32) * gate).astype(BF16)
    rows[...] = dot(grad_outer, out_w()[...], ((1,), (1,))) * u_gain()[...]
    for jh in range(4):
        block = jnp.concatenate(
            [rows[pl.ds(4 * jh + jl, 32, stride=16), :] for jl in range(4)], axis=0
        )
        eg_out[pl.ds(jh * 128, 128), :] = block.T


def tri_back_kernel(tri, eg, out, tri_rows, d_rows):
    tri_rows[...] = tri[...].astype(F32)
    for jh in range(4):
        value = tri_rows[pl.ds(jh, 128, stride=4), :]
        centre = jnp.mean(value, axis=0, keepdims=True)
        shifted = value - centre
        inverse = lax.rsqrt(jnp.mean(shifted * shifted, axis=0, keepdims=True) + epsilon)
        scaled = shifted * inverse
        grad_hat = eg[pl.ds(jh * 128, 128), :]
        first_mean = jnp.mean(grad_hat, axis=0, keepdims=True)
        second_mean = jnp.mean(grad_hat * scaled, axis=0, keepdims=True)
        d_rows[pl.ds(jh, 128, stride=4), :] = inverse * (
            grad_hat - first_mean - scaled * second_mean
        )
    out[...] = d_rows[...].astype(BF16)


def tile_kernel(
    tri, gain, bias, u_gain, u_bias, gate_w, tile, out_w, cotangent,
    update, grad_tile, mark, tri_rows, run_rows,
):
    gain, bias, gate_w = gain(), bias(), gate_w()
    mark[...] = jnp.zeros_like(mark)
    tri_rows[...] = tri[...].astype(F32)
    for jh in range(4):
        block = tri_rows[pl.ds(jh, 128, stride=4), :].T
        for jl in range(4):
            run_rows[pl.ds(4 * jh + jl, 32, stride=16), :] = block[jl * 32 : jl * 32 + 32, :]
    tri_scaled, _ = stats(run_rows[...])
    outer = dot((tri_scaled * u_gain()[...] + u_bias()[...]).astype(BF16), out_w()[...])
    gate, scaled, inverse = gate_of(tile(), gate_w, gain, bias)
    update[...] = (gate * outer).astype(BF16)
    grad_gate = (cotangent()[...].astype(F32) * outer * gate * (1.0 - gate)).astype(BF16)
    grad_norm = dot(grad_gate, gate_w[...], ((1,), (1,)))
    grad_tile[...] = norm_back(scaled, inverse, grad_norm, gain[...]).astype(BF16)


def factor_kernel(
    gain, bias, w_left, slab, w_right, column,
    kept,
):
    g, b = gain()[...], bias()[...]
    w_left, slab, w_right, column = w_left(), slab(), w_right(), column()
    for n, weights in enumerate((w_left, w_right)):
        for half in range(2):
            kept[pl.ds(9216 + (2 * n + half) * 128, 128), :] = weights[
                :, half * 128 : half * 128 + 128
            ]
    for step in range(24):
        source, weights = (slab, w_left) if step < 8 else (column, w_right)
        start = step * 96 if step < 8 else (step - 8) * 96
        linear, sigma, scaled, inverse = edges(source[pl.ds(start, 96), :], weights[...], g, b)
        values = (sigma, linear * sigma * (1.0 - sigma), inverse * g, scaled)
        for plane, value in enumerate(values):
            kept[pl.ds(plane * 2304 + step * 96, 96), :] = value.astype(BF16)


def third_product_kernel(core, d_got, left, mark, d_tri, d_right, rows, d_rows):
    group = lane_group((32, 128))
    rows[...] = d_got[...].astype(F32)
    for jh in range(4):
        parts = [rows[pl.ds(zl * 128 + jh, 32, stride=4), :] for zl in range(4)]
        for jl in range(4):
            d_rows[pl.ds((4 * jh + jl) * 32, 32), :] = gathered(parts, (jl,) * 4, range(4), group)
    d_now = d_rows[...].astype(BF16)
    d_tri[...] = d_now
    for zl in range(4):
        block = dot(d_now, left_block(left, zl, 1 - core[0]), ((1,), (1,)))
        d_right[pl.ds(zl * 512, 512), :] = block.astype(BF16)


def fourth_product_kernel(core, d_tri, right_own, right_other, left, base, d_left):
    d_now = d_tri[...]
    d_t = d_now.astype(F32).T.astype(BF16)
    for zl in range(4):
        for right, which in ((right_own, core[0]), (right_other, 1 - core[0])):
            block = dot(d_t, right[pl.ds(zl * 512, 512), :]).T
            start = pl.multiple_of((2 * zl + which) * 96, 32)
            d_left[pl.ds(start, 96), :] = block[:96, :]
    group = lane_group((32, 128))

    def left_part(k):
        return d_left[pl.ds(k, 32, stride=24), :]

    for zl in range(4):
        block = dot(d_now, left_block(left, zl, core[0]), ((1,), (1,)))
        for r in range(ROWS):
            if r < 16:
                merged = jnp.where(
                    group == 3, moved(left_part(r), zl, 3), block[r * 32 : r * 32 + 32, :]
                )
            else:
                parts = [left_part(tail_k(r, q)) for q in range(4)]
                merged = gathered(parts, (zl,) * 4, range(4), group)
            base[pl.ds(zl * 32 * ROWS + r, 32, stride=ROWS), :] = merged


def fifth_product_kernel(come, base, out, rows):
    for zl in range(4):
        for r in range(ROWS):
            target = pl.ds(zl * 32 * ROWS + r, 32, stride=ROWS)
            if r < 16:
                rows[target, :] = come[pl.ds(zl * 512 + r * 32, 32), :].astype(F32)
            else:
                rows[target, :] = jnp.zeros((32, 128), F32)
    out[...] = (base[...] + rows[...]).astype(BF16)


def edges_back(grad_edge, start, weights, kept):
    sigma, slope, scale, scaled = (
        kept[pl.ds(plane * 2304 + start, 96), :].astype(F32) for plane in range(4)
    )
    joined = jnp.concatenate([grad_edge * sigma, grad_edge * slope], axis=1)
    grad_hat = dot(joined.astype(BF16), weights, ((1,), (1,))) * scale
    first_mean = jnp.mean(grad_hat, axis=-1, keepdims=True)
    second_mean = jnp.mean(grad_hat * scaled, axis=-1, keepdims=True)
    return (grad_hat - first_mean - scaled * second_mean).astype(BF16)


def project_back_kernel(
    back, kept, grad_slab, grad_column, chunks, left_rows
):
    w_left, w_right = (
        jnp.concatenate(
            [kept[pl.ds(9216 + (2 * n + half) * 128, 128), :] for half in range(2)], axis=1
        )
        for n in range(2)
    )
    chunks[...] = back[...].astype(F32)
    for r in range(ROWS):
        block = chunks[pl.ds(r, 128, stride=ROWS), :].T
        if r < 16:
            left_rows[pl.ds(r, 32, stride=24), :] = block[96:, :]
            grad_column[pl.ds(r * 96, 96), :] = edges_back(
                block[:96, :], 768 + r * 96, w_right, kept
            )
        else:
            for q in range(4):
                left_rows[pl.ds(tail_k(r, q), 32, stride=24), :] = block[q * 32 : q * 32 + 32, :]
    for step in range(8):
        rows = pl.ds(step * 96, 96)
        grad_slab[rows, :] = edges_back(left_rows[rows, :], step * 96, w_left, kept)


VMEM = pl.BlockSpec(memory_space=pltpu.VMEM)
SMEM = pl.BlockSpec(memory_space=pltpu.SMEM)
HBM = pl.BlockSpec(memory_space=pltpu.HBM)


class Staged:
    def __init__(self, copy, ref):
        self.copy, self.ref, self.waiting = copy, ref, True
        copy.start()

    def __call__(self):
        if self.waiting:
            self.copy.wait()
            self.waiting = False
        return self.ref


def run(kernel, name, outs, scratch, args, fetched=(), limit=16, cost=2_000_000):
    cuts = [len(args), len(fetched), len(outs), len(scratch), len(fetched)]

    def body(*refs):
        groups, at = [], 0
        for size in cuts:
            groups.append(refs[at : at + size])
            at += size
        plain, sources, results, work, stages = groups
        staged = [
            Staged(pltpu.make_async_copy(source, stage, refs[-1].at[n]), stage)
            for n, (source, stage) in enumerate(zip(sources, stages))
        ]
        kernel(*plain, *staged, *results, *work)
        for item in staged:
            item()

    scratches = [pltpu.VMEM((n, 128), F32) for n in scratch]
    scratches += [pltpu.VMEM(a.shape, a.dtype) for a in fetched]
    if fetched:
        scratches.append(pltpu.SemaphoreType.DMA((len(fetched),)))
    return pl.pallas_call(
        body,
        name=name,
        out_shape=[jax.ShapeDtypeStruct(s, t) for s, t in outs],
        in_specs=[SMEM if a.dtype == jnp.int32 else VMEM for a in args] + [HBM] * len(fetched),
        out_specs=[VMEM] * len(outs),
        scratch_shapes=scratches,
        cost_estimate=pl.CostEstimate(flops=50 * cost, bytes_accessed=cost, transcendentals=0),
        compiler_params=pltpu.CompilerParams(vmem_limit_bytes=limit and limit << 20),
    )(*args, *[pltpu.with_memory_space_constraint(a, pltpu.HBM) for a in fetched])


def shuffled(array):
    rows = array.shape[0] // 128
    shape = (128, rows // 2, 2, 128) if rows == ROWS else (128, rows, 128)
    return lax.all_to_all(array.reshape(shape), SPLIT, 0, 0, tiled=True).reshape(array.shape)


def swapped(array):
    return lax.ppermute(array, "co", [(0, 1), (1, 0)])


def shards(
    slab_rows,
    column_rows,
    pair_tile,
    cotangent,
    weights_left,
    weights_right,
    gate_weight,
    out_weight,
    input_gain,
    input_bias,
    update_gain,
    update_bias,
):
    core = lax.axis_index("co").astype(jnp.int32).reshape(1)
    slab = slab_rows.reshape(768, 128)
    column = column_rows.reshape(1536, 128)
    tile = pair_tile.reshape(512, 128)
    cots = cotangent.reshape(512, 128)
    gain, bias, u_gain, u_bias = (
        v.reshape(1, 128) for v in (input_gain, input_bias, update_gain, update_bias)
    )
    (sent,) = run(
        project_kernel, "project", [((128 * ROWS, 128), BF16)], [768, 128 * ROWS], (),
        (gain, bias, weights_left, slab, weights_right, column), limit=16,
    )
    got = shuffled(sent)
    (eg,) = run(
        gate_kernel, "gate", [((512, 128), F32)], [512], (),
        (gain, bias, u_gain, gate_weight, tile, out_weight, cots),
    )
    come = swapped(got)
    left, right_own, partial = run(
        first_product_kernel, "product_one",
        [((768, 128), BF16), ((2048, 128), BF16), ((512, 128), F32)],
        [128 * ROWS, 768], (core, got),
    )
    right_other, tri_sent = run(
        second_product_kernel, "product_two",
        [((2048, 128), BF16), ((512, 128), BF16)], [128 * ROWS, 512], (core, come, left, partial),
    )
    tri = shuffled(tri_sent)
    (d_sent,) = run(tri_back_kernel, "tri_back", [((512, 128), BF16)], [512, 512], (tri, eg))
    d_got = shuffled(d_sent)
    update, grad_tile, mark = run(
        tile_kernel, "tile", [((512, 128), BF16)] * 2 + [((8, 128), F32)], [512, 512], (tri,),
        (gain, bias, u_gain, u_bias, gate_weight, tile, out_weight, cots),
    )
    d_tri, d_right_other = run(
        third_product_kernel, "product_three",
        [((512, 128), BF16), ((2048, 128), BF16)], [512, 512], (core, d_got, left, mark),
    )
    d_right_come = swapped(d_right_other)
    (base,) = run(
        fourth_product_kernel, "product_four", [((128 * ROWS, 128), F32)], [768],
        (core, d_tri, right_own, right_other, left),
    )
    (back_sent,) = run(
        fifth_product_kernel, "product_five", [((128 * ROWS, 128), BF16)], [128 * ROWS],
        (d_right_come, base),
    )
    back = shuffled(back_sent)
    (kept,) = run(
        factor_kernel, "factors",
        [((4 * 2304 + 512, 128), BF16)],
        [], (), (gain, bias, weights_left, slab, weights_right, column),
    )
    grad_slab, grad_column = run(
        project_back_kernel, "project_back",
        [((768, 128), BF16), ((1536, 128), BF16)], [128 * ROWS, 768], (back, kept),
    )
    return (
        update.reshape(pair_tile.shape),
        grad_slab.reshape(slab_rows.shape),
        grad_column.reshape(column_rows.shape),
        grad_tile.reshape(pair_tile.shape),
    )


def solution(mesh):
    finer = Mesh(mesh.devices.reshape(4, 2, 4, 4, 2), ("zl", "co", "y", "x", "zh"))
    row_spec = P(IA, JA, None)
    column_spec = P(JA, IA, None)
    in_specs = (row_spec, column_spec, row_spec, row_spec) + (P(),) * 8
    return jax.shard_map(
        shards,
        mesh=finer,
        in_specs=in_specs,
        out_specs=(row_spec, row_spec, column_spec, row_spec),
        check_vma=False,
    )
```

```python
import functools

import jax
import jax.numpy as jnp
from jax import lax
from jax.experimental import pallas as pl
from jax.experimental.pallas import tpu as pltpu
from jax.sharding import Mesh
from jax.sharding import PartitionSpec as P

IA = ("zl", "co")
JA = ("y", "x", "zh")
SPLIT = ("zl", "y", "x", "zh")

epsilon = 1e-05
F32 = jnp.float32
BF16 = jnp.bfloat16


ROWS = 18
SPAN = 384


def stats(values):
    centre = jnp.mean(values, axis=-1, keepdims=True)
    shifted = values - centre
    inverse = lax.rsqrt(jnp.mean(shifted * shifted, axis=-1, keepdims=True) + epsilon)
    return shifted * inverse, inverse


def norm_back(scaled, inverse, grad_out, gain):
    grad_hat = grad_out * gain
    first_mean = jnp.mean(grad_hat, axis=-1, keepdims=True)
    second_mean = jnp.mean(grad_hat * scaled, axis=-1, keepdims=True)
    return inverse * (grad_hat - first_mean - scaled * second_mean)


def dot(a, b, dims=((1,), (0,))):
    return lax.dot_general(a, b, (dims, ((), ())), preferred_element_type=F32)


def edges(rows, weights, gain, bias):
    scaled, inverse = stats(rows.astype(F32))
    hidden = dot((scaled * gain + bias).astype(BF16), weights)
    return hidden[:, :128], jax.nn.sigmoid(hidden[:, 128:]), scaled, inverse


def lane_group(shape):
    return lax.broadcasted_iota(jnp.int32, shape, 1) // 32


def moved(block, source, target):
    shift = ((target - source) * 32) % 128
    return block if shift == 0 else pltpu.roll(block, shift, 1)


def tail_k(r, g):
    return 16 + 4 * (r - 16) + g


def project_kernel(gain, bias, w_left, slab, w_right, column, out, left_rows, chunks):
    g, b = gain()[...], bias()[...]
    w_left, slab = w_left(), slab()
    for step in range(768 // SPAN):
        rows = pl.ds(step * SPAN, SPAN)
        linear, sigma, _, _ = edges(slab[rows, :], w_left[...], g, b)
        left_rows[rows, :] = sigma * linear

    def left_part(k):
        return left_rows[pl.ds(k, 32, stride=24), :]

    w_right, column = w_right(), column()
    values = None
    for r in range(ROWS):
        if r < 16:
            at = r * 96 % SPAN
            if at == 0:
                linear, sigma, _, _ = edges(column[pl.ds(r * 96, SPAN), :], w_right[...], g, b)
                values = sigma * linear
            parts = [values[at : at + 96, :], left_part(r)]
        else:
            parts = [left_part(tail_k(r, q)) for q in range(4)]
        chunks[pl.ds(r, 128, stride=ROWS), :] = jnp.concatenate(parts, axis=0).T
    out[...] = chunks[...].astype(BF16)


def gathered(parts, sources, targets, group):
    merged = None
    for part, source, target in zip(parts, sources, targets):
        piece = moved(part, source, target)
        merged = piece if merged is None else jnp.where(group == target, piece, merged)
    return merged


def padded(rows):
    return jnp.concatenate([rows, jnp.zeros((32, 128), BF16)], axis=0)


def left_block(left, zl, core):
    start = pl.multiple_of((2 * zl + core) * 96, 32)
    return padded(left[pl.ds(start, 96), :])


def first_product_kernel(core, got, left, right, partial, rows, left_rows):
    group = lane_group((32, 128))
    rows[...] = got[...].astype(F32)
    left_of(rows, left_rows, group)
    for zl in range(4):
        for r in range(16):
            right[pl.ds(zl * 512 + r * 32, 32), :] = rows[
                pl.ds(zl * 32 * ROWS + r, 32, stride=ROWS), :
            ].astype(BF16)
    left[...] = left_rows[...].astype(BF16)
    total = None
    for zl in range(4):
        term = dot(right[pl.ds(zl * 512, 512), :], left_block(left, zl, core[0]))
        total = term if total is None else total + term
    partial[...] = total


def second_product_kernel(core, come, left, partial, mark, right, out, rows, sent):
    rows[...] = come[...].astype(F32)
    acc = partial[...]
    for zl in range(4):
        for r in range(16):
            right[pl.ds(zl * 512 + r * 32, 32), :] = rows[
                pl.ds(zl * 32 * ROWS + r, 32, stride=ROWS), :
            ].astype(BF16)
        acc = acc + dot(right[pl.ds(zl * 512, 512), :], left_block(left, zl, 1 - core[0]))
    group = lane_group((32, 128))
    for jh in range(4):
        parts = [acc[(4 * jh + jl) * 32 : (4 * jh + jl + 1) * 32, :] for jl in range(4)]
        for zl in range(4):
            sent[pl.ds(zl * 128 + jh, 32, stride=4), :] = gathered(
                parts, (zl,) * 4, range(4), group
            )
    out[...] = sent[...].astype(BF16)


def gate_of(tile, gate_w, gain, bias):
    scaled, inverse = stats(tile[...].astype(F32))
    hidden = dot((scaled * gain[...] + bias[...]).astype(BF16), gate_w[...])
    return jax.nn.sigmoid(hidden), scaled, inverse


def gate_kernel(gain, bias, u_gain, gate_w, tile, out_w, cotangent, eg_out, rows):
    gate, _, _ = gate_of(tile, gate_w, gain, bias)
    grad_outer = (cotangent[...].astype(F32) * gate).astype(BF16)
    rows[...] = dot(grad_outer, out_w[...], ((1,), (1,))) * u_gain[...]
    for jh in range(4):
        block = jnp.concatenate(
            [rows[pl.ds(4 * jh + jl, 32, stride=16), :] for jl in range(4)], axis=0
        )
        eg_out[pl.ds(jh * 128, 128), :] = block.T


def tri_back_kernel(tri, eg, out, tri_rows, d_rows):
    tri_rows[...] = tri[...].astype(F32)
    for jh in range(4):
        value = tri_rows[pl.ds(jh, 128, stride=4), :]
        centre = jnp.mean(value, axis=0, keepdims=True)
        shifted = value - centre
        inverse = lax.rsqrt(jnp.mean(shifted * shifted, axis=0, keepdims=True) + epsilon)
        scaled = shifted * inverse
        grad_hat = eg[pl.ds(jh * 128, 128), :]
        first_mean = jnp.mean(grad_hat, axis=0, keepdims=True)
        second_mean = jnp.mean(grad_hat * scaled, axis=0, keepdims=True)
        d_rows[pl.ds(jh, 128, stride=4), :] = inverse * (
            grad_hat - first_mean - scaled * second_mean
        )
    out[...] = d_rows[...].astype(BF16)


def tile_kernel(
    tri, gain, bias, u_gain, u_bias, gate_w, tile, out_w, cotangent,
    update, grad_tile, tri_rows, run_rows,
):
    gain, bias, gate_w = gain(), bias(), gate_w()
    tri_rows[...] = tri[...].astype(F32)
    for jh in range(4):
        block = tri_rows[pl.ds(jh, 128, stride=4), :].T
        for jl in range(4):
            run_rows[pl.ds(4 * jh + jl, 32, stride=16), :] = block[jl * 32 : jl * 32 + 32, :]
    tri_scaled, _ = stats(run_rows[...])
    outer = dot((tri_scaled * u_gain()[...] + u_bias()[...]).astype(BF16), out_w()[...])
    gate, scaled, inverse = gate_of(tile(), gate_w, gain, bias)
    update[...] = (gate * outer).astype(BF16)
    grad_gate = (cotangent()[...].astype(F32) * outer * gate * (1.0 - gate)).astype(BF16)
    grad_norm = dot(grad_gate, gate_w[...], ((1,), (1,)))
    grad_tile[...] = norm_back(scaled, inverse, grad_norm, gain[...]).astype(BF16)


def factor_kernel(
    gain, bias, w_left, slab, w_right, column,
    kept,
):
    g, b = gain()[...], bias()[...]
    w_left, slab, w_right, column = w_left(), slab(), w_right(), column()
    for n, weights in enumerate((w_left, w_right)):
        for half in range(2):
            kept[pl.ds(9216 + (2 * n + half) * 128, 128), :] = weights[
                :, half * 128 : half * 128 + 128
            ]
    for step in range(24):
        source, weights = (slab, w_left) if step < 8 else (column, w_right)
        start = step * 96 if step < 8 else (step - 8) * 96
        linear, sigma, scaled, inverse = edges(source[pl.ds(start, 96), :], weights[...], g, b)
        values = (sigma, linear * sigma * (1.0 - sigma), inverse * g, scaled)
        for plane, value in enumerate(values):
            kept[pl.ds(plane * 2304 + step * 96, 96), :] = value.astype(BF16)


def left_of(rows, left_rows, group):
    for r in range(ROWS):
        parts = [rows[pl.ds(zl * 32 * ROWS + r, 32, stride=ROWS), :] for zl in range(4)]
        for q in (3,) if r < 16 else range(4):
            k = r if r < 16 else tail_k(r, q)
            left_rows[pl.ds(k, 32, stride=24), :] = gathered(parts, (q,) * 4, range(4), group)


def tri_of(got, rows, d_rows, group):
    rows[...] = got[...].astype(F32)
    for jh in range(4):
        parts = [rows[pl.ds(zl * 128 + jh, 32, stride=4), :] for zl in range(4)]
        for jl in range(4):
            d_rows[pl.ds((4 * jh + jl) * 32, 32), :] = gathered(parts, (jl,) * 4, range(4), group)
    return d_rows[...].astype(BF16)


def third_product_kernel(
    core, d_got, left, come, right_own, right_other,
    base, left_come, rows, d_rows, d_left, come_rows, left_rows,
):
    group = lane_group((32, 128))
    d_now = tri_of(d_got, rows, d_rows, group)
    d_t = d_rows[...].T.astype(BF16)
    for zl in range(4):
        for right, which in ((right_own, core[0]), (right_other, 1 - core[0])):
            block = dot(d_t, right[pl.ds(zl * 512, 512), :]).T
            start = pl.multiple_of((2 * zl + which) * 96, 32)
            d_left[pl.ds(start, 96), :] = block[:96, :]

    def left_part(k):
        return d_left[pl.ds(k, 32, stride=24), :]

    for zl in range(4):
        block = dot(d_now, left_block(left, zl, core[0]), ((1,), (1,)))
        for r in range(ROWS):
            if r < 16:
                merged = jnp.where(
                    group == 3, moved(left_part(r), zl, 3), block[r * 32 : r * 32 + 32, :]
                )
            else:
                parts = [left_part(tail_k(r, q)) for q in range(4)]
                merged = gathered(parts, (zl,) * 4, range(4), group)
            base[pl.ds(zl * 32 * ROWS + r, 32, stride=ROWS), :] = merged
    come_rows[...] = come[...].astype(F32)
    left_of(come_rows, left_rows, group)
    left_come[...] = left_rows[...].astype(BF16)


def fourth_product_kernel(core, d_come, left_come, base, out, rows, d_rows, sent):
    group = lane_group((32, 128))
    d_now = tri_of(d_come, rows, d_rows, group)
    for zl in range(4):
        block = dot(d_now, left_block(left_come, zl, core[0]), ((1,), (1,)))
        for r in range(ROWS):
            target = pl.ds(zl * 32 * ROWS + r, 32, stride=ROWS)
            if r < 16:
                sent[target, :] = base[target, :] + block[r * 32 : r * 32 + 32, :]
            else:
                sent[target, :] = base[target, :]
    out[...] = sent[...].astype(BF16)


def edges_back(grad_edge, start, weights, kept):
    sigma, slope, scale, scaled = (
        kept[pl.ds(plane * 2304 + start, SPAN), :].astype(F32) for plane in range(4)
    )
    joined = jnp.concatenate([grad_edge * sigma, grad_edge * slope], axis=1)
    grad_hat = dot(joined.astype(BF16), weights, ((1,), (1,))) * scale
    first_mean = jnp.mean(grad_hat, axis=-1, keepdims=True)
    second_mean = jnp.mean(grad_hat * scaled, axis=-1, keepdims=True)
    return (grad_hat - first_mean - scaled * second_mean).astype(BF16)


def project_back_kernel(
    back, kept, grad_slab, grad_column, chunks, left_rows
):
    w_left, w_right = (
        jnp.concatenate(
            [kept[pl.ds(9216 + (2 * n + half) * 128, 128), :] for half in range(2)], axis=1
        )
        for n in range(2)
    )
    chunks[...] = back[...].astype(F32)
    held = []
    for r in range(ROWS):
        block = chunks[pl.ds(r, 128, stride=ROWS), :].T
        if r < 16:
            left_rows[pl.ds(r, 32, stride=24), :] = block[96:, :]
            held.append(block[:96, :])
            if len(held) * 96 == SPAN:
                start = (r + 1) * 96 - SPAN
                grad_column[pl.ds(start, SPAN), :] = edges_back(
                    jnp.concatenate(held, axis=0), 768 + start, w_right, kept
                )
                held = []
        else:
            for q in range(4):
                left_rows[pl.ds(tail_k(r, q), 32, stride=24), :] = block[q * 32 : q * 32 + 32, :]
    for step in range(768 // SPAN):
        rows = pl.ds(step * SPAN, SPAN)
        grad_slab[rows, :] = edges_back(left_rows[rows, :], step * SPAN, w_left, kept)


VMEM = pl.BlockSpec(memory_space=pltpu.VMEM)
SMEM = pl.BlockSpec(memory_space=pltpu.SMEM)
HBM = pl.BlockSpec(memory_space=pltpu.HBM)


class Staged:
    def __init__(self, copy, ref):
        self.copy, self.ref, self.waiting = copy, ref, True
        copy.start()

    def __call__(self):
        if self.waiting:
            self.copy.wait()
            self.waiting = False
        return self.ref


def run(kernel, name, outs, scratch, args, fetched=(), limit=16, cost=2_000_000):
    cuts = [len(args), len(fetched), len(outs), len(scratch), len(fetched)]

    def body(*refs):
        groups, at = [], 0
        for size in cuts:
            groups.append(refs[at : at + size])
            at += size
        plain, sources, results, work, stages = groups
        staged = [
            Staged(pltpu.make_async_copy(source, stage, refs[-1].at[n]), stage)
            for n, (source, stage) in enumerate(zip(sources, stages))
        ]
        kernel(*plain, *staged, *results, *work)
        for item in staged:
            item()

    scratches = [pltpu.VMEM((n, 128), F32) for n in scratch]
    scratches += [pltpu.VMEM(a.shape, a.dtype) for a in fetched]
    if fetched:
        scratches.append(pltpu.SemaphoreType.DMA((len(fetched),)))
    return pl.pallas_call(
        body,
        name=name,
        out_shape=[jax.ShapeDtypeStruct(s, t) for s, t in outs],
        in_specs=[SMEM if a.dtype == jnp.int32 else VMEM for a in args] + [HBM] * len(fetched),
        out_specs=[VMEM] * len(outs),
        scratch_shapes=scratches,
        cost_estimate=pl.CostEstimate(flops=50 * cost, bytes_accessed=cost, transcendentals=0),
        compiler_params=pltpu.CompilerParams(vmem_limit_bytes=limit and limit << 20),
    )(*args, *[pltpu.with_memory_space_constraint(a, pltpu.HBM) for a in fetched])


def shuffled(array):
    rows = array.shape[0] // 128
    shape = (128, rows // 2, 2, 128) if rows == ROWS else (128, rows, 128)
    return lax.all_to_all(array.reshape(shape), SPLIT, 0, 0, tiled=True).reshape(array.shape)


def swapped(array):
    return lax.ppermute(array, "co", [(0, 1), (1, 0)])


def shards(
    slab_rows,
    column_rows,
    pair_tile,
    cotangent,
    weights_left,
    weights_right,
    gate_weight,
    out_weight,
    input_gain,
    input_bias,
    update_gain,
    update_bias,
):
    core = lax.axis_index("co").astype(jnp.int32).reshape(1)
    slab = slab_rows.reshape(768, 128)
    column = column_rows.reshape(1536, 128)
    tile = pair_tile.reshape(512, 128)
    cots = cotangent.reshape(512, 128)
    gain, bias, u_gain, u_bias = (
        v.reshape(1, 128) for v in (input_gain, input_bias, update_gain, update_bias)
    )
    (sent,) = run(
        project_kernel, "project", [((128 * ROWS, 128), BF16)], [768, 128 * ROWS], (),
        (gain, bias, weights_left, slab, weights_right, column), limit=16,
    )
    got = shuffled(sent)
    (eg,) = run(
        gate_kernel, "gate", [((512, 128), F32)], [512],
        (gain, bias, u_gain, gate_weight, tile, out_weight, cots),
    )
    come = swapped(got)
    left, right_own, partial = run(
        first_product_kernel, "product_one",
        [((768, 128), BF16), ((2048, 128), BF16), ((512, 128), F32)],
        [128 * ROWS, 768], (core, got),
    )
    right_other, tri_sent = run(
        second_product_kernel, "product_two",
        [((2048, 128), BF16), ((512, 128), BF16)], [128 * ROWS, 512], (core, come, left, partial, eg),
    )
    tri = shuffled(tri_sent)
    (d_sent,) = run(tri_back_kernel, "tri_back", [((512, 128), BF16)], [512, 512], (tri, eg))
    d_got = shuffled(d_sent)
    update, grad_tile = run(
        tile_kernel, "tile", [((512, 128), BF16)] * 2, [512, 512], (tri,),
        (gain, bias, u_gain, u_bias, gate_weight, tile, out_weight, cots),
    )
    d_come = swapped(d_got)
    base, left_come = run(
        third_product_kernel, "product_three",
        [((128 * ROWS, 128), F32), ((768, 128), BF16)], [512, 512, 768, 128 * ROWS, 768],
        (core, d_got, left, come, right_own, right_other),
    )
    (back_sent,) = run(
        fourth_product_kernel, "product_four", [((128 * ROWS, 128), BF16)],
        [512, 512, 128 * ROWS], (core, d_come, left_come, base),
    )
    back = shuffled(back_sent)
    (kept,) = run(
        factor_kernel, "factors",
        [((4 * 2304 + 512, 128), BF16)],
        [], (), (gain, bias, weights_left, slab, weights_right, column),
    )
    grad_slab, grad_column = run(
        project_back_kernel, "project_back",
        [((768, 128), BF16), ((1536, 128), BF16)], [128 * ROWS, 768], (back, kept),
    )
    return (
        update.reshape(pair_tile.shape),
        grad_slab.reshape(slab_rows.shape),
        grad_column.reshape(column_rows.shape),
        grad_tile.reshape(pair_tile.shape),
    )


def solution(mesh):
    finer = Mesh(mesh.devices.reshape(4, 2, 4, 4, 2), ("zl", "co", "y", "x", "zh"))
    row_spec = P(IA, JA, None)
    column_spec = P(JA, IA, None)
    in_specs = (row_spec, column_spec, row_spec, row_spec) + (P(),) * 8
    return jax.shard_map(
        shards,
        mesh=finer,
        in_specs=in_specs,
        out_specs=(row_spec, row_spec, column_spec, row_spec),
        check_vma=False,
    )
```

```python
import functools

import jax
import jax.numpy as jnp
from jax import lax
from jax.experimental import pallas as pl
from jax.experimental.pallas import tpu as pltpu
from jax.sharding import Mesh
from jax.sharding import PartitionSpec as P

IA = ("zl", "co")
JA = ("y", "x", "zh")
SPLIT = ("zl", "y", "x", "zh")

epsilon = 1e-05
F32 = jnp.float32
BF16 = jnp.bfloat16


ROWS = 18
SPAN = 384


def stats(values):
    centre = jnp.mean(values, axis=-1, keepdims=True)
    shifted = values - centre
    inverse = lax.rsqrt(jnp.mean(shifted * shifted, axis=-1, keepdims=True) + epsilon)
    return shifted * inverse, inverse


def norm_back(scaled, inverse, grad_out, gain):
    grad_hat = grad_out * gain
    first_mean = jnp.mean(grad_hat, axis=-1, keepdims=True)
    second_mean = jnp.mean(grad_hat * scaled, axis=-1, keepdims=True)
    return inverse * (grad_hat - first_mean - scaled * second_mean)


def dot(a, b, dims=((1,), (0,))):
    return lax.dot_general(a, b, (dims, ((), ())), preferred_element_type=F32)


def edges(rows, weights, gain, bias):
    scaled, inverse = stats(rows.astype(F32))
    hidden = dot((scaled * gain + bias).astype(BF16), weights)
    return hidden[:, :128], jax.nn.sigmoid(hidden[:, 128:]), scaled, inverse


def lane_group(shape):
    return lax.broadcasted_iota(jnp.int32, shape, 1) // 32


def moved(block, source, target):
    shift = ((target - source) * 32) % 128
    return block if shift == 0 else pltpu.roll(block, shift, 1)


def tail_k(r, g):
    return 16 + 4 * (r - 16) + g


def project_kernel(gain, bias, w_left, slab, w_right, column, out, left_rows, chunks):
    g, b = gain()[...], bias()[...]
    w_left, slab = w_left(), slab()
    for step in range(768 // SPAN):
        rows = pl.ds(step * SPAN, SPAN)
        linear, sigma, _, _ = edges(slab[rows, :], w_left[...], g, b)
        left_rows[rows, :] = sigma * linear

    def left_part(k):
        return left_rows[pl.ds(k, 32, stride=24), :]

    w_right, column = w_right(), column()
    values = None
    for r in range(ROWS):
        if r < 16:
            at = r * 96 % SPAN
            if at == 0:
                linear, sigma, _, _ = edges(column[pl.ds(r * 96, SPAN), :], w_right[...], g, b)
                values = sigma * linear
            parts = [values[at : at + 96, :], left_part(r)]
        else:
            parts = [left_part(tail_k(r, q)) for q in range(4)]
        chunks[pl.ds(r, 128, stride=ROWS), :] = jnp.concatenate(parts, axis=0).T
    out[...] = chunks[...].astype(BF16)


def gathered(parts, sources, targets, group):
    merged = None
    for part, source, target in zip(parts, sources, targets):
        piece = moved(part, source, target)
        merged = piece if merged is None else jnp.where(group == target, piece, merged)
    return merged


def padded(rows):
    return jnp.concatenate([rows, jnp.zeros((32, 128), BF16)], axis=0)


def left_block(left, zl, core):
    start = pl.multiple_of((2 * zl + core) * 96, 32)
    return padded(left[pl.ds(start, 96), :])


def first_product_kernel(core, got, left, right, partial, rows, left_rows):
    group = lane_group((32, 128))
    rows[...] = got[...].astype(F32)
    left_of(rows, left_rows, group)
    for zl in range(4):
        for r in range(16):
            right[pl.ds(zl * 512 + r * 32, 32), :] = rows[
                pl.ds(zl * 32 * ROWS + r, 32, stride=ROWS), :
            ].astype(BF16)
    left[...] = left_rows[...].astype(BF16)
    total = None
    for zl in range(4):
        term = dot(right[pl.ds(zl * 512, 512), :], left_block(left, zl, core[0]))
        total = term if total is None else total + term
    partial[...] = total


def second_product_kernel(core, come, left, partial, mark, right, out, rows, sent):
    rows[...] = come[...].astype(F32)
    acc = partial[...]
    for zl in range(4):
        for r in range(16):
            right[pl.ds(zl * 512 + r * 32, 32), :] = rows[
                pl.ds(zl * 32 * ROWS + r, 32, stride=ROWS), :
            ].astype(BF16)
        acc = acc + dot(right[pl.ds(zl * 512, 512), :], left_block(left, zl, 1 - core[0]))
    group = lane_group((32, 128))
    for jh in range(4):
        parts = [acc[(4 * jh + jl) * 32 : (4 * jh + jl + 1) * 32, :] for jl in range(4)]
        for zl in range(4):
            sent[pl.ds(zl * 128 + jh, 32, stride=4), :] = gathered(
                parts, (zl,) * 4, range(4), group
            )
    out[...] = sent[...].astype(BF16)


def gate_of(tile, gate_w, gain, bias):
    scaled, inverse = stats(tile[...].astype(F32))
    hidden = dot((scaled * gain[...] + bias[...]).astype(BF16), gate_w[...])
    return jax.nn.sigmoid(hidden), scaled, inverse


def gate_kernel(gain, bias, u_gain, gate_w, tile, out_w, cotangent, eg_out, rows):
    gate, _, _ = gate_of(tile, gate_w, gain, bias)
    grad_outer = (cotangent[...].astype(F32) * gate).astype(BF16)
    rows[...] = dot(grad_outer, out_w[...], ((1,), (1,))) * u_gain[...]
    for jh in range(4):
        block = jnp.concatenate(
            [rows[pl.ds(4 * jh + jl, 32, stride=16), :] for jl in range(4)], axis=0
        )
        eg_out[pl.ds(jh * 128, 128), :] = block.T


def tri_back_kernel(tri, eg, out, tri_rows, d_rows):
    tri_rows[...] = tri[...].astype(F32)
    for jh in range(4):
        value = tri_rows[pl.ds(jh, 128, stride=4), :]
        centre = jnp.mean(value, axis=0, keepdims=True)
        shifted = value - centre
        inverse = lax.rsqrt(jnp.mean(shifted * shifted, axis=0, keepdims=True) + epsilon)
        scaled = shifted * inverse
        grad_hat = eg[pl.ds(jh * 128, 128), :]
        first_mean = jnp.mean(grad_hat, axis=0, keepdims=True)
        second_mean = jnp.mean(grad_hat * scaled, axis=0, keepdims=True)
        d_rows[pl.ds(jh, 128, stride=4), :] = inverse * (
            grad_hat - first_mean - scaled * second_mean
        )
    out[...] = d_rows[...].astype(BF16)


def tile_kernel(
    tri, gain, bias, u_gain, u_bias, gate_w, tile, out_w, cotangent,
    update, grad_tile, tri_rows, run_rows,
):
    gain, bias, gate_w = gain(), bias(), gate_w()
    tri_rows[...] = tri[...].astype(F32)
    for jh in range(4):
        block = tri_rows[pl.ds(jh, 128, stride=4), :].T
        for jl in range(4):
            run_rows[pl.ds(4 * jh + jl, 32, stride=16), :] = block[jl * 32 : jl * 32 + 32, :]
    tri_scaled, _ = stats(run_rows[...])
    outer = dot((tri_scaled * u_gain()[...] + u_bias()[...]).astype(BF16), out_w()[...])
    gate, scaled, inverse = gate_of(tile(), gate_w, gain, bias)
    update[...] = (gate * outer).astype(BF16)
    grad_gate = (cotangent()[...].astype(F32) * outer * gate * (1.0 - gate)).astype(BF16)
    grad_norm = dot(grad_gate, gate_w[...], ((1,), (1,)))
    grad_tile[...] = norm_back(scaled, inverse, grad_norm, gain[...]).astype(BF16)


def factor_kernel(
    gain, bias, w_left, slab, w_right, column,
    kept,
):
    g, b = gain()[...], bias()[...]
    w_left, slab, w_right, column = w_left(), slab(), w_right(), column()
    for n, weights in enumerate((w_left, w_right)):
        for half in range(2):
            kept[pl.ds(9216 + (2 * n + half) * 128, 128), :] = weights[
                :, half * 128 : half * 128 + 128
            ]
    for step in range(24):
        source, weights = (slab, w_left) if step < 8 else (column, w_right)
        start = step * 96 if step < 8 else (step - 8) * 96
        linear, sigma, scaled, inverse = edges(source[pl.ds(start, 96), :], weights[...], g, b)
        values = (sigma, linear * sigma * (1.0 - sigma), inverse * g, scaled)
        for plane, value in enumerate(values):
            kept[pl.ds(plane * 2304 + step * 96, 96), :] = value.astype(BF16)


def left_of(rows, left_rows, group):
    for r in range(ROWS):
        parts = [rows[pl.ds(zl * 32 * ROWS + r, 32, stride=ROWS), :] for zl in range(4)]
        for q in (3,) if r < 16 else range(4):
            k = r if r < 16 else tail_k(r, q)
            left_rows[pl.ds(k, 32, stride=24), :] = gathered(parts, (q,) * 4, range(4), group)


def tri_of(got, rows, d_rows, group):
    rows[...] = got[...].astype(F32)
    for jh in range(4):
        parts = [rows[pl.ds(zl * 128 + jh, 32, stride=4), :] for zl in range(4)]
        for jl in range(4):
            d_rows[pl.ds((4 * jh + jl) * 32, 32), :] = gathered(parts, (jl,) * 4, range(4), group)
    return d_rows[...].astype(BF16)


def third_product_kernel(
    core, d_got, left, come, right_own, right_other,
    base, left_come, rows, d_rows, d_left, come_rows, left_rows,
):
    group = lane_group((32, 128))
    d_now = tri_of(d_got, rows, d_rows, group)
    d_t = d_rows[...].T.astype(BF16)
    for zl in range(4):
        for right, which in ((right_own, core[0]), (right_other, 1 - core[0])):
            block = dot(d_t, right[pl.ds(zl * 512, 512), :]).T
            start = pl.multiple_of((2 * zl + which) * 96, 32)
            d_left[pl.ds(start, 96), :] = block[:96, :]

    def left_part(k):
        return d_left[pl.ds(k, 32, stride=24), :]

    for zl in range(4):
        block = dot(d_now, left_block(left, zl, core[0]), ((1,), (1,)))
        for r in range(ROWS):
            if r < 16:
                merged = jnp.where(
                    group == 3, moved(left_part(r), zl, 3), block[r * 32 : r * 32 + 32, :]
                )
            else:
                parts = [left_part(tail_k(r, q)) for q in range(4)]
                merged = gathered(parts, (zl,) * 4, range(4), group)
            base[pl.ds(zl * 32 * ROWS + r, 32, stride=ROWS), :] = merged
    come_rows[...] = come[...].astype(F32)
    left_of(come_rows, left_rows, group)
    left_come[...] = left_rows[...].astype(BF16)


def fourth_product_kernel(core, d_come, left_come, base, out, rows, d_rows, sent):
    group = lane_group((32, 128))
    d_now = tri_of(d_come, rows, d_rows, group)
    for zl in range(4):
        block = dot(d_now, left_block(left_come, zl, core[0]), ((1,), (1,)))
        for r in range(ROWS):
            target = pl.ds(zl * 32 * ROWS + r, 32, stride=ROWS)
            if r < 16:
                sent[target, :] = base[target, :] + block[r * 32 : r * 32 + 32, :]
            else:
                sent[target, :] = base[target, :]
        out.put(zl * 32 * ROWS, sent[pl.ds(zl * 32 * ROWS, 32 * ROWS), :].astype(BF16))


def edges_back(grad_edge, start, weights, kept):
    sigma, slope, scale, scaled = (
        kept[pl.ds(plane * 2304 + start, SPAN), :].astype(F32) for plane in range(4)
    )
    joined = jnp.concatenate([grad_edge * sigma, grad_edge * slope], axis=1)
    grad_hat = dot(joined.astype(BF16), weights, ((1,), (1,))) * scale
    first_mean = jnp.mean(grad_hat, axis=-1, keepdims=True)
    second_mean = jnp.mean(grad_hat * scaled, axis=-1, keepdims=True)
    return (grad_hat - first_mean - scaled * second_mean).astype(BF16)


def project_back_kernel(
    back, kept, grad_slab, grad_column, chunks, left_rows
):
    w_left, w_right = (
        jnp.concatenate(
            [kept[pl.ds(9216 + (2 * n + half) * 128, 128), :] for half in range(2)], axis=1
        )
        for n in range(2)
    )
    chunks[...] = back[...].astype(F32)
    held = []
    for r in range(ROWS):
        block = chunks[pl.ds(r, 128, stride=ROWS), :].T
        if r < 16:
            left_rows[pl.ds(r, 32, stride=24), :] = block[96:, :]
            held.append(block[:96, :])
            if len(held) * 96 == SPAN:
                start = (r + 1) * 96 - SPAN
                grad_column.put(
                    start, edges_back(jnp.concatenate(held, axis=0), 768 + start, w_right, kept)
                )
                held = []
        else:
            for q in range(4):
                left_rows[pl.ds(tail_k(r, q), 32, stride=24), :] = block[q * 32 : q * 32 + 32, :]
    for step in range(768 // SPAN):
        rows = pl.ds(step * SPAN, SPAN)
        grad_slab.put(step * SPAN, edges_back(left_rows[rows, :], step * SPAN, w_left, kept))


VMEM = pl.BlockSpec(memory_space=pltpu.VMEM)
SMEM = pl.BlockSpec(memory_space=pltpu.SMEM)
HBM = pl.BlockSpec(memory_space=pltpu.HBM)


class Staged:
    def __init__(self, copy, ref):
        self.copy, self.ref, self.waiting = copy, ref, True
        copy.start()

    def __call__(self):
        if self.waiting:
            self.copy.wait()
            self.waiting = False
        return self.ref


class Streamed:
    def __init__(self, out, stage, sems, first):
        self.out, self.stage, self.sems, self.at, self.copies = out, stage, sems, first, []

    def put(self, start, value):
        rows = pl.ds(start, value.shape[0])
        self.stage[rows, :] = value
        copy = pltpu.make_async_copy(
            self.stage.at[rows, :], self.out.at[rows, :], self.sems.at[self.at]
        )
        copy.start()
        self.at += 1
        self.copies.append(copy)


def run(kernel, name, outs, scratch, args, fetched=(), limit=16, cost=2_000_000, streamed=False):
    staged_outs = outs if streamed else []
    cuts = [len(args), len(fetched), len(outs), len(scratch), len(fetched), len(staged_outs)]

    def body(*refs):
        groups, at = [], 0
        for size in cuts:
            groups.append(refs[at : at + size])
            at += size
        plain, sources, results, work, stages, out_stages = groups
        if streamed:
            results = [
                Streamed(out, stage, refs[-1], 8 * n)
                for n, (out, stage) in enumerate(zip(results, out_stages))
            ]
        staged = [
            Staged(pltpu.make_async_copy(source, stage, refs[-1].at[n]), stage)
            for n, (source, stage) in enumerate(zip(sources, stages))
        ]
        kernel(*plain, *staged, *results, *work)
        for item in staged:
            item()
        if streamed:
            for result in results:
                for copy in result.copies:
                    copy.wait()

    scratches = [pltpu.VMEM((n, 128), F32) for n in scratch]
    scratches += [pltpu.VMEM(a.shape, a.dtype) for a in fetched]
    scratches += [pltpu.VMEM(shape, dtype) for shape, dtype in staged_outs]
    if fetched:
        scratches.append(pltpu.SemaphoreType.DMA((len(fetched),)))
    if streamed:
        scratches.append(pltpu.SemaphoreType.DMA((8 * len(outs),)))
    return pl.pallas_call(
        body,
        name=name,
        out_shape=[jax.ShapeDtypeStruct(s, t) for s, t in outs],
        in_specs=[SMEM if a.dtype == jnp.int32 else VMEM for a in args] + [HBM] * len(fetched),
        out_specs=[HBM if streamed else VMEM] * len(outs),
        scratch_shapes=scratches,
        cost_estimate=pl.CostEstimate(flops=50 * cost, bytes_accessed=cost, transcendentals=0),
        compiler_params=pltpu.CompilerParams(vmem_limit_bytes=limit and limit << 20),
    )(*args, *[pltpu.with_memory_space_constraint(a, pltpu.HBM) for a in fetched])


def shuffled(array):
    rows = array.shape[0] // 128
    shape = (128, rows // 2, 2, 128) if rows == ROWS else (128, rows, 128)
    return lax.all_to_all(array.reshape(shape), SPLIT, 0, 0, tiled=True).reshape(array.shape)


def swapped(array):
    return lax.ppermute(array, "co", [(0, 1), (1, 0)])


def shards(
    slab_rows,
    column_rows,
    pair_tile,
    cotangent,
    weights_left,
    weights_right,
    gate_weight,
    out_weight,
    input_gain,
    input_bias,
    update_gain,
    update_bias,
):
    core = lax.axis_index("co").astype(jnp.int32).reshape(1)
    slab = slab_rows.reshape(768, 128)
    column = column_rows.reshape(1536, 128)
    tile = pair_tile.reshape(512, 128)
    cots = cotangent.reshape(512, 128)
    gain, bias, u_gain, u_bias = (
        v.reshape(1, 128) for v in (input_gain, input_bias, update_gain, update_bias)
    )
    (sent,) = run(
        project_kernel, "project", [((128 * ROWS, 128), BF16)], [768, 128 * ROWS], (),
        (gain, bias, weights_left, slab, weights_right, column), limit=16,
    )
    got = shuffled(sent)
    (eg,) = run(
        gate_kernel, "gate", [((512, 128), F32)], [512],
        (gain, bias, u_gain, gate_weight, tile, out_weight, cots),
    )
    come = swapped(got)
    left, right_own, partial = run(
        first_product_kernel, "product_one",
        [((768, 128), BF16), ((2048, 128), BF16), ((512, 128), F32)],
        [128 * ROWS, 768], (core, got),
    )
    right_other, tri_sent = run(
        second_product_kernel, "product_two",
        [((2048, 128), BF16), ((512, 128), BF16)], [128 * ROWS, 512], (core, come, left, partial, eg),
    )
    tri = shuffled(tri_sent)
    (d_sent,) = run(tri_back_kernel, "tri_back", [((512, 128), BF16)], [512, 512], (tri, eg))
    d_got = shuffled(d_sent)
    update, grad_tile = run(
        tile_kernel, "tile", [((512, 128), BF16)] * 2, [512, 512], (tri,),
        (gain, bias, u_gain, u_bias, gate_weight, tile, out_weight, cots),
    )
    d_come = swapped(d_got)
    base, left_come = run(
        third_product_kernel, "product_three",
        [((128 * ROWS, 128), F32), ((768, 128), BF16)], [512, 512, 768, 128 * ROWS, 768],
        (core, d_got, left, come, right_own, right_other),
    )
    (back_sent,) = run(
        fourth_product_kernel, "product_four", [((128 * ROWS, 128), BF16)],
        [512, 512, 128 * ROWS], (core, d_come, left_come, base), streamed=True,
    )
    back = shuffled(back_sent)
    (kept,) = run(
        factor_kernel, "factors",
        [((4 * 2304 + 512, 128), BF16)],
        [], (), (gain, bias, weights_left, slab, weights_right, column),
    )
    grad_slab, grad_column = run(
        project_back_kernel, "project_back",
        [((768, 128), BF16), ((1536, 128), BF16)], [128 * ROWS, 768], (back, kept), streamed=True,
    )
    return (
        update.reshape(pair_tile.shape),
        grad_slab.reshape(slab_rows.shape),
        grad_column.reshape(column_rows.shape),
        grad_tile.reshape(pair_tile.shape),
    )


def solution(mesh):
    finer = Mesh(mesh.devices.reshape(4, 2, 4, 4, 2), ("zl", "co", "y", "x", "zh"))
    row_spec = P(IA, JA, None)
    column_spec = P(JA, IA, None)
    in_specs = (row_spec, column_spec, row_spec, row_spec) + (P(),) * 8
    return jax.shard_map(
        shards,
        mesh=finer,
        in_specs=in_specs,
        out_specs=(row_spec, row_spec, column_spec, row_spec),
        check_vma=False,
    )
```
